32 devices in a mesh: chan: 8 (over y, x, core), stn: 4 (over z).
Axes of the slice: x: 2, y: 2, z: 4, core: 2. Of those that a mesh axis runs over, the one named last changes fastest.
Arguments:
- measured_correlation: float32 [8, 8, 4096], P('chan', None, 'stn'), may hold values from -3 to 3
- model_correlation: float32 [8, 8, 16, 4096], P('chan', None, None, 'stn'), may hold values from -1.0606601 to 1.0606601
- source_pointing: int32 [16, 1], replicated, may hold values from 0 to 7
- antenna_pairs: int32 [2, 4096], P(None, 'stn'), may hold values from 0 to 511, as said below
- starting_jones_matrices: float32 [8, 8, 8, 512], P('chan'), may hold values from -1 to 2
- starting_polynomial_terms: float32 [3, 8, 8, 512], replicated, may hold values from -1 to 2
- starting_lagrange_scaled: float32 [8, 8, 8, 512], P('chan'), may hold values from -1.5 to 1.5
- augmented_lagrange_rhos: float32 [8], replicated, may hold values from 0.5 to 4
Outputs:
- solved_gains: float32 [8, 8, 8, 512], P('chan', None, None, 'stn')
- solved_dual: float32 [8, 8, 8, 512], P('chan', None, None, 'stn')
- fit_coeffs: float32 [3, 8, 8, 512], P(None, None, None, 'stn')
The draws below stay inside these ranges and needn't reach their ends.
Inputs may be any that keep to these rules, and one draw needn't show every extreme that they name: `antenna_pairs`: row 0 holds a baseline's first station and row 1 its second, which differs from the first. The first station of every baseline in the i-th aligned block of 1024 baselines lies among stations i * 128 to (i + 1) * 128 - 1. `source_pointing`: every direction holds at least one component.
All inputs are finite; a program needn't handle non-finite values.
Results may differ from the reference program's by a relative error of at most 0.0001.
Values sent between devices are 32-bit elements; how exact they have to be, the bound alone decides.
No kernel may reach another device: no remote copies, remote signals or barrier semaphores. Data moves between devices by JAX's collectives and lax.ppermute only.
A program may use at most 64 MiB of HBM per device.

```python
import math
import jax
import jax.numpy as jnp
from jax import lax

STATION_COUNT = 512
CALIB_PATHS = 8
SKY_COMPONENTS = 16
TERMS = 3
STEPS = 2
INNER = 2
BL_DEV = 1024
FREQ_CHANNELS = 8
BASELINE_COUNT = 4096
BLOCK_STATIONS = 128


def draw_antenna_pairs(key, part):
    row_index = jnp.arange(BASELINE_COUNT, dtype=jnp.int32)
    block_holder = row_index // BL_DEV
    first_key = jax.random.fold_in(key, 11)
    second_key = jax.random.fold_in(key, 12)
    first_station = block_holder * BLOCK_STATIONS + jax.random.randint(first_key, (BASELINE_COUNT,), 0, BLOCK_STATIONS, dtype=jnp.int32)
    second_station = (first_station + 1 + jax.random.randint(second_key, (BASELINE_COUNT,), 0, STATION_COUNT - 1, dtype=jnp.int32)) % STATION_COUNT
    return jnp.stack([first_station, second_station], axis=0)


def draw_starting_jones_matrices(key, part):
    full_shape = (FREQ_CHANNELS, 8, CALIB_PATHS, STATION_COUNT)
    sub_key = jax.random.fold_in(key, 21)
    jitter_part = jnp.clip(jax.random.normal(sub_key, full_shape, jnp.float32), -4.0, 4.0) * 0.25
    component = jnp.arange(8, dtype=jnp.int32)
    identity = ((component == 0) | (component == 3)).astype(jnp.float32)[None, :, None, None]
    return identity + jitter_part


def draw_starting_polynomial_terms(key, part):
    full_shape = (TERMS, 8, CALIB_PATHS, STATION_COUNT)
    sub_key = jax.random.fold_in(key, 31)
    jitter_part = jnp.clip(jax.random.normal(sub_key, full_shape, jnp.float32), -4.0, 4.0) * 0.25
    component = jnp.arange(8, dtype=jnp.int32)
    degree_ids = jnp.arange(TERMS, dtype=jnp.int32)
    identity = (((component == 0) | (component == 3))[None, :] & (degree_ids == 0)[:, None]).astype(jnp.float32)
    return identity[:, :, None, None] + jitter_part


def block_levels(own_key, shape, cuts, low, top_value):
    level, own = 1.0, jax.random.fold_in(own_key, 6)
    for dim, shards_of in cuts:
        steps = jnp.exp(jax.random.uniform(jax.random.fold_in(own, dim), (shards_of,), jnp.float32, low / len(cuts), top_value / len(cuts)))
        level = level * jnp.repeat(steps, shape[dim] // shards_of).reshape([-1 if axis == dim else 1 for axis in range(len(shape))])
    return level


def different_ones(key, rows, number_of, top, lift):
    ranking = jax.random.permutation(jax.random.fold_in(key, 1), number_of)
    favour = ranking
    for power in range(3):
        favour = favour * favour // number_of
    favour = favour * lift // number_of
    chance = jax.random.randint(jax.random.fold_in(key, 2), (rows, number_of), 0, 4096) + favour
    holders = jax.random.permutation(jax.random.fold_in(key, 3), rows)[jnp.arange(number_of) % rows]
    chance = jnp.where(jnp.arange(rows)[:, None] == holders[None, :], 1 << 14, chance)
    score = chance * number_of + jnp.arange(number_of)
    return lax.top_k(score.astype(jnp.int32), top)[1].astype(jnp.int32)


def scatter_about(own_key, dims, deviation, limit, cuts=(), held_as=jnp.bfloat16):
    drawn = jax.random.normal(own_key, dims, jnp.float32) * deviation
    if len(cuts) > 0:
        drawn = block_levels(own_key, dims, cuts, -0.22, 0.18) * drawn
    return jnp.clip(drawn, min=-limit, max=limit).astype(held_as)


def setup_inputs(seed: int = 0) -> dict:
    arg_keys = jax.random.split(jax.random.key(seed), 9)
    measured_correlation = scatter_about(arg_keys[0], (FREQ_CHANNELS, 8, BASELINE_COUNT), 0.5, 3.0, ((0, 8), (2, 4)), jnp.float32)
    model_correlation = scatter_about(arg_keys[1], (FREQ_CHANNELS, 8, SKY_COMPONENTS, BASELINE_COUNT), (0.5 * STATION_COUNT ** 0.5 * BASELINE_COUNT ** -0.5), 1.0606601, ((0, 8), (3, 4)), jnp.float32)
    source_pointing = different_ones(arg_keys[2], SKY_COMPONENTS, CALIB_PATHS, 1, 1024)
    antenna_pairs = draw_antenna_pairs(jax.random.fold_in(arg_keys[8], 71), 0)
    starting_jones_matrices = draw_starting_jones_matrices(jax.random.fold_in(arg_keys[8], 71), 0)
    starting_polynomial_terms = draw_starting_polynomial_terms(jax.random.fold_in(arg_keys[8], 71), 0)
    starting_lagrange_scaled = scatter_about(arg_keys[6], (FREQ_CHANNELS, 8, CALIB_PATHS, STATION_COUNT), 0.3, 1.5, ((0, 8),), jnp.float32)
    augmented_lagrange_rhos = jnp.clip(jnp.exp(jax.random.uniform(arg_keys[7], (CALIB_PATHS,), jnp.float32, math.log(0.5), math.log(4.0))), 0.5, 4.0)
    return dict(measured_correlation=measured_correlation, model_correlation=model_correlation, source_pointing=source_pointing, antenna_pairs=antenna_pairs, starting_jones_matrices=starting_jones_matrices, starting_polynomial_terms=starting_polynomial_terms, starting_lagrange_scaled=starting_lagrange_scaled, augmented_lagrange_rhos=augmented_lagrange_rhos)


student_nu = 2.0
squared_tolerance = 1e-06
highest = lax.Precision.HIGHEST

def entries(stacked):
    return [(stacked[slot_idx], stacked[4 + slot_idx]) for slot_idx in range(4)]

def assemble(matrix):
    return jnp.stack([matrix[slot_idx][0] for slot_idx in range(4)] + [matrix[slot_idx][1] for slot_idx in range(4)], axis=0)

def flatten(matrix):
    return [matrix[slot_idx][0] for slot_idx in range(4)] + [matrix[slot_idx][1] for slot_idx in range(4)]

def multiply_pair(first_pair, second_pair):
    return (first_pair[0] * second_pair[0] - first_pair[1] * second_pair[1], first_pair[0] * second_pair[1] + first_pair[1] * second_pair[0])

def add_pair(first_pair, second_pair):
    return (first_pair[0] + second_pair[0], first_pair[1] + second_pair[1])

def conjugate(value_pair):
    return (value_pair[0], -value_pair[1])

def matrix_product(factor_one, factor_two):
    return [add_pair(multiply_pair(factor_one[0], factor_two[0]), multiply_pair(factor_one[1], factor_two[2])), add_pair(multiply_pair(factor_one[0], factor_two[1]), multiply_pair(factor_one[1], factor_two[3])), add_pair(multiply_pair(factor_one[2], factor_two[0]), multiply_pair(factor_one[3], factor_two[2])), add_pair(multiply_pair(factor_one[2], factor_two[1]), multiply_pair(factor_one[3], factor_two[3]))]

def adjoint(matrix):
    return [conjugate(matrix[0]), conjugate(matrix[2]), conjugate(matrix[1]), conjugate(matrix[3])]

def gram_parts(matrix):
    upper_sum = matrix[0][0] * matrix[0][0] + matrix[0][1] * matrix[0][1] + matrix[1][0] * matrix[1][0] + matrix[1][1] * matrix[1][1]
    lower_sum = matrix[2][0] * matrix[2][0] + matrix[2][1] * matrix[2][1] + matrix[3][0] * matrix[3][0] + matrix[3][1] * matrix[3][1]
    cross_term = add_pair(multiply_pair(matrix[0], conjugate(matrix[2])), multiply_pair(matrix[1], conjugate(matrix[3])))
    return [upper_sum, lower_sum, cross_term[0], cross_term[1]]

def basis_table(channel_count):
    frequency = (2.0 * jnp.arange(channel_count, dtype=jnp.float32) + 1.0) / channel_count - 1.0
    columns = []
    for degree in range(TERMS):
        column = frequency ** degree
        for earlier in columns:
            column = column - jnp.sum(earlier * column) / channel_count * earlier
        column = column / jnp.sqrt(jnp.sum(column * column) / channel_count)
        columns.append(column)
    return jnp.stack(columns, axis=1)

def combine_sources(cohere_f, source_pointing):
    member = (source_pointing[:, 0][:, None] == jnp.arange(CALIB_PATHS, dtype=jnp.int32)[None, :]).astype(jnp.float32)
    return jnp.einsum('csb,sk->ckb', cohere_f, member, precision=highest)

def channel_state(vis_f, cohere_dir, spectral_jones_matrices, antenna_pairs):
    coherent = entries(cohere_dir)
    first_gain = entries(spectral_jones_matrices[:, :, antenna_pairs[0]])
    second_gain = entries(spectral_jones_matrices[:, :, antenna_pairs[1]])
    toward_first = matrix_product(coherent, adjoint(second_gain))
    own_terms = matrix_product(first_gain, toward_first)
    observed = entries(vis_f)
    residual = [(observed[slot_idx][0] - lax.optimization_barrier(jnp.sum(own_terms[slot_idx][0], axis=0)), observed[slot_idx][1] - lax.optimization_barrier(jnp.sum(own_terms[slot_idx][1], axis=0))) for slot_idx in range(4)]
    energy = residual[0][0] * residual[0][0] + residual[0][1] * residual[0][1]
    for slot_idx in range(1, 4):
        energy = energy + residual[slot_idx][0] * residual[slot_idx][0] + residual[slot_idx][1] * residual[slot_idx][1]
    return (residual, own_terms, toward_first, first_gain, coherent, energy)

def channel_sums(chan_state, weight, antenna_pairs, station_count):
    residual, own_terms, toward_first, first_gain, coherent, energy = chan_state
    target = [add_pair((residual[slot_idx][0][None], residual[slot_idx][1][None]), own_terms[slot_idx]) for slot_idx in range(4)]
    back_terms = matrix_product(first_gain, coherent)
    first_parts = jnp.stack(gram_parts(toward_first) + flatten(matrix_product(target, adjoint(toward_first))), axis=0) * weight
    second_parts = jnp.stack(gram_parts(adjoint(back_terms)) + flatten(matrix_product(adjoint(target), back_terms)), axis=0) * weight
    zero_sums = jnp.zeros((12, first_parts.shape[1], station_count), jnp.float32)
    return zero_sums.at[:, :, antenna_pairs[0]].add(first_parts).at[:, :, antenna_pairs[1]].add(second_parts)

def jones_estimator(least_squares_equations, pivot_spectral_point, spectral_jones_matrices, augmented_lagrange_rhos):
    augmented_rho_factor = augmented_lagrange_rhos[:, None]
    diag_one = least_squares_equations[0] + augmented_rho_factor
    diag_two = least_squares_equations[1] + augmented_rho_factor
    determinant = diag_one * diag_two - least_squares_equations[2] * least_squares_equations[2] - least_squares_equations[3] * least_squares_equations[3]
    zero_part = jnp.zeros_like(determinant)
    inverse = [(diag_two / determinant, zero_part), (-least_squares_equations[2] / determinant, -least_squares_equations[3] / determinant), (-least_squares_equations[2] / determinant, least_squares_equations[3] / determinant), (diag_one / determinant, zero_part)]
    right_side = entries(least_squares_equations[4:] + augmented_rho_factor[None] * pivot_spectral_point)
    solution = assemble(matrix_product(right_side, inverse))
    return 0.5 * (spectral_jones_matrices + solution)

def plain_python_iterate(measured_correlation, model_correlation, source_pointing, antenna_pairs, present_jones_matrix, pivot_antenna, augmented_lagrange_rhos):

    def energy_of(channel_items):
        vis_f, cohere_f, spectral_jones_matrices = channel_items
        chan_state = channel_state(vis_f, combine_sources(cohere_f, source_pointing), spectral_jones_matrices, antenna_pairs)
        return jnp.sum(chan_state[5])
    summed_energy = jnp.sum(lax.map(energy_of, (measured_correlation, model_correlation, present_jones_matrix)))
    mean_square = summed_energy / (FREQ_CHANNELS * BASELINE_COUNT) + squared_tolerance

    def update_of(channel_items):
        vis_f, cohere_f, spectral_jones_matrices, pivot_spectral_point = channel_items
        chan_state = channel_state(vis_f, combine_sources(cohere_f, source_pointing), spectral_jones_matrices, antenna_pairs)
        weight = (student_nu + 2.0) / (student_nu + chan_state[5] / mean_square)
        least_squares_equations = channel_sums(chan_state, weight, antenna_pairs, STATION_COUNT)
        return jones_estimator(least_squares_equations, pivot_spectral_point, spectral_jones_matrices, augmented_lagrange_rhos)
    return lax.map(update_of, (measured_correlation, model_correlation, present_jones_matrix, pivot_antenna))

def reference(measured_correlation, model_correlation, source_pointing, antenna_pairs, starting_jones_matrices, starting_polynomial_terms, starting_lagrange_scaled, augmented_lagrange_rhos):
    basis = basis_table(FREQ_CHANNELS)
    consensus = jnp.einsum('ft,tcks->fcks', basis, starting_polynomial_terms, precision=highest)
    present_jones_matrix = starting_jones_matrices
    dual_now = starting_lagrange_scaled
    fit_now = starting_polynomial_terms
    for step_idx in range(STEPS):
        pivot_antenna = consensus - dual_now
        for inner_idx in range(INNER):
            present_jones_matrix = plain_python_iterate(measured_correlation, model_correlation, source_pointing, antenna_pairs, present_jones_matrix, pivot_antenna, augmented_lagrange_rhos)
        fit_now = jnp.einsum('ft,fcks->tcks', basis, present_jones_matrix + dual_now, precision=highest) / FREQ_CHANNELS
        consensus = jnp.einsum('ft,tcks->fcks', basis, fit_now, precision=highest)
        dual_now = dual_now + present_jones_matrix - consensus
    return (present_jones_matrix, dual_now, fit_now)
```

```python
from functools import partial

import jax
import jax.numpy as jnp
from jax import lax
from jax.experimental import pallas as pl
from jax.experimental.pallas import tpu as pltpu
from jax.sharding import PartitionSpec as P

TERMS = 3
STEPS = 2
INNER = 2
COMPS = 8
LANES = 128

student_nu = 2.0
squared_tolerance = 1e-06
f32 = jnp.float32
bf16 = jnp.bfloat16


def cmul(a, b):
    return (a[0] * b[0] - a[1] * b[1], a[0] * b[1] + a[1] * b[0])


def cadd(a, b):
    return (a[0] + b[0], a[1] + b[1])


def conj(a):
    return (a[0], -a[1])


def mmul(a, b):
    return [
        cadd(cmul(a[0], b[0]), cmul(a[1], b[2])),
        cadd(cmul(a[0], b[1]), cmul(a[1], b[3])),
        cadd(cmul(a[2], b[0]), cmul(a[3], b[2])),
        cadd(cmul(a[2], b[1]), cmul(a[3], b[3])),
    ]


def adj(m):
    return [conj(m[0]), conj(m[2]), conj(m[1]), conj(m[3])]


def flat(m):
    return [m[i][0] for i in range(4)] + [m[i][1] for i in range(4)]


def square(a):
    return a[0] * a[0] + a[1] * a[1]


def gram(m):
    cross = cadd(cmul(m[0], conj(m[2])), cmul(m[1], conj(m[3])))
    return [
        square(m[0]) + square(m[1]),
        square(m[2]) + square(m[3]),
        cross[0],
        cross[1],
    ]


def basis_table(channel_count):
    frequency = (2.0 * jnp.arange(channel_count, dtype=f32) + 1.0) / channel_count - 1.0
    columns = []
    for degree in range(TERMS):
        column = frequency**degree
        for earlier in columns:
            column = column - jnp.sum(earlier * column) / channel_count * earlier
        column = column / jnp.sqrt(jnp.sum(column * column) / channel_count)
        columns.append(column)
    return jnp.stack(columns, axis=1)


def split(x):
    hi = x.astype(bf16)
    lo = (x - hi.astype(f32)).astype(bf16)
    return hi, lo


def load(ref, paths, lanes):
    rows = [ref[c * paths : (c + 1) * paths, lanes] for c in range(COMPS)]
    return [(rows[i], rows[4 + i]) for i in range(4)]


def combine_kernel(point_ref, model_ref, vis_ref, pair_ref, out_ref, *, paths, comps):
    width = out_ref.shape[1]
    which = lax.broadcasted_iota(jnp.int32, (paths, width), 0)
    for c in range(COMPS):
        total = jnp.zeros((paths, width), f32)
        for s in range(comps):
            row = model_ref[c * comps + s : c * comps + s + 1, :]
            total = total + jnp.where(which == point_ref[s], row, 0.0)
        out_ref[c * paths : (c + 1) * paths, :] = total
    base = COMPS * paths
    out_ref[base : base + COMPS, :] = vis_ref[...]
    out_ref[base + COMPS : base + COMPS + 2, :] = pair_ref[...].astype(f32)


class Plan:
    def __init__(self, paths, stations, blocks, width):
        self.paths, self.stations = paths, stations
        self.blocks, self.width = blocks, width
        self.rows = COMPS * paths
        own = stations // blocks
        self.own = own
        self.window = min(stations, max(own, LANES))
        self.starts = [i * own // self.window * self.window for i in range(blocks)]


def make_onehots(plan, msg_ref, ohp_ref, ohq_ref):
    width, base = plan.width, plan.rows + COMPS
    for i in range(plan.blocks):
        lanes = slice(i * width, (i + 1) * width)
        first = msg_ref[base : base + 1, lanes].astype(jnp.int32) - plan.starts[i]
        second = msg_ref[base + 1 : base + 2, lanes].astype(jnp.int32)
        pos = lax.broadcasted_iota(jnp.int32, (plan.window, width), 0)
        ohp_ref[:, lanes] = jnp.where(pos == first, 1.0, 0.0).astype(bf16)
        pos = lax.broadcasted_iota(jnp.int32, (plan.stations, width), 0)
        ohq_ref[:, lanes] = jnp.where(pos == second, 1.0, 0.0).astype(bf16)


def residuals(plan, gains, msg_ref, ohp_ref, ohq_ref, x_ref, y_ref, h_ref, e_ref, jp_ref, jq_ref):
    paths, rows, width = plan.paths, plan.rows, plan.width
    hi, lo = split(gains)
    both = jnp.concatenate([hi, lo], axis=0)
    total = jnp.zeros((1, LANES), f32)
    for i in range(plan.blocks):
        block = slice(i * width, (i + 1) * width)
        window = slice(plan.starts[i], plan.starts[i] + plan.window)
        got = jnp.dot(both, ohq_ref[:, block], preferred_element_type=f32)
        jq_ref[...] = got[:rows] + got[rows:]
        got = jnp.dot(both[:, window], ohp_ref[:, block], preferred_element_type=f32)
        jp_ref[...] = got[:rows] + got[rows:]

        def piece(t, carry):
            here = pl.ds(pl.multiple_of(t * LANES, LANES), LANES)
            there = pl.ds(pl.multiple_of(i * width + t * LANES, LANES), LANES)
            coherent = load(msg_ref, paths, there)
            y = mmul(coherent, adj(load(jq_ref, paths, here)))
            for c, v in enumerate(flat(y)):
                y_ref[c * paths : (c + 1) * paths, there] = v
            first = load(jp_ref, paths, here)
            g = flat(mmul(first, y))
            energy = jnp.zeros((1, LANES), f32)
            for c in range(COMPS):
                r = msg_ref[rows + c : rows + c + 1, there] - jnp.sum(g[c], axis=0, keepdims=True)
                energy = energy + r * r
                x_ref[c * paths : (c + 1) * paths, there] = r + g[c]
            for c, v in enumerate(flat(mmul(first, coherent))):
                h_ref[c * paths : (c + 1) * paths, there] = v
            e_ref[0:1, there] = energy
            return carry + energy

        total = lax.fori_loop(0, width // LANES, piece, total)
    return total


def normal_sums(plan, noise, ohp_ref, ohq_ref, x_ref, y_ref, h_ref, e_ref, fp_ref, sp_ref, acc_ref):
    paths, width = plan.paths, plan.width
    half = 12 * paths
    contract = (((1,), (1,)), ((), ()))
    for i in range(plan.blocks):
        block = slice(i * width, (i + 1) * width)
        window = slice(plan.starts[i], plan.starts[i] + plan.window)

        def piece(t, carry):
            here = pl.ds(pl.multiple_of(t * LANES, LANES), LANES)
            there = pl.ds(pl.multiple_of(i * width + t * LANES, LANES), LANES)
            weight = (student_nu + 2.0) / (student_nu + e_ref[0:1, there] / noise)
            weight = jnp.broadcast_to(weight, (paths, LANES))
            x = [(a * weight, b * weight) for a, b in load(x_ref, paths, there)]
            y = load(y_ref, paths, there)
            parts = [v * weight for v in gram(y)] + flat(mmul(x, adj(y)))
            hi, lo = split(jnp.concatenate(parts, axis=0))
            fp_ref[0:half, here] = hi
            fp_ref[half : 2 * half, here] = lo
            h = load(h_ref, paths, there)
            parts = [v * weight for v in gram(adj(h))] + flat(mmul(adj(x), h))
            hi, lo = split(jnp.concatenate(parts, axis=0))
            sp_ref[0:half, here] = hi
            sp_ref[half : 2 * half, here] = lo
            return carry

        lax.fori_loop(0, width // LANES, piece, 0)
        got = lax.dot_general(sp_ref[...], ohq_ref[:, block], contract, preferred_element_type=f32)
        got = got[:half] + got[half:]
        if i == 0:
            acc_ref[...] = got
        else:
            acc_ref[...] += got
        got = lax.dot_general(fp_ref[...], ohp_ref[:, block], contract, preferred_element_type=f32)
        acc_ref[:, window] += got[:half] + got[half:]


def solve(plan, acc_ref, anchor, gains, rho):
    paths = plan.paths
    part = [acc_ref[c * paths : (c + 1) * paths, :] for c in range(12)]
    a, d = part[0] + rho, part[1] + rho
    inv = 1.0 / (a * d - part[2] * part[2] - part[3] * part[3])
    a, d, c0, c1 = a * inv, d * inv, part[2] * inv, part[3] * inv
    rhs = [part[4 + c] + rho * anchor[c * paths : (c + 1) * paths] for c in range(COMPS)]
    out = [None] * COMPS
    for row in (0, 2):
        u = (rhs[row], rhs[4 + row])
        v = (rhs[row + 1], rhs[5 + row])
        left = cmul(v, (c0, -c1))
        right = cmul(u, (c0, c1))
        out[row], out[4 + row] = u[0] * d - left[0], u[1] * d - left[1]
        out[row + 1], out[5 + row] = v[0] * a - right[0], v[1] * a - right[1]
    return 0.5 * (gains + jnp.concatenate(out, axis=0))


def noise_of(energy, count):
    per_lane = jnp.sum(energy, axis=0, keepdims=True)
    return jnp.sum(per_lane, axis=1, keepdims=True) / count + squared_tolerance


def params(limit=24 << 20):
    return pltpu.CompilerParams(vmem_limit_bytes=limit)


VM = pl.BlockSpec(memory_space=pltpu.VMEM)
SM = pl.BlockSpec(memory_space=pltpu.SMEM)


def first_kernel(gain_ref, msg_ref, ohp_ref, ohq_ref, x_ref, y_ref, h_ref, e_ref, sum_ref,
                 jp_ref, jq_ref, *, plan):
    make_onehots(plan, msg_ref, ohp_ref, ohq_ref)
    total = residuals(plan, gain_ref[...], msg_ref, ohp_ref, ohq_ref, x_ref, y_ref, h_ref, e_ref,
                      jp_ref, jq_ref)
    sum_ref[...] = jnp.broadcast_to(total, sum_ref.shape)


def rho_column(rho_ref, paths, width):
    which = lax.broadcasted_iota(jnp.int32, (paths, width), 0)
    out = jnp.zeros((paths, width), f32)
    for k in range(paths):
        out = jnp.where(which == k, rho_ref[k], out)
    return out


def middle_kernel(rho_ref, gain_ref, anchor_ref, energy_ref, msg_ref, ohp_ref, ohq_ref,
                  x_ref, y_ref, h_ref, e_ref,
                  gain_out, x_out, y_out, h_out, e_out, sum_ref,
                  jp_ref, jq_ref, fp_ref, sp_ref, acc_ref, *, plan, count):
    noise = noise_of(energy_ref[...], count)
    normal_sums(plan, noise, ohp_ref, ohq_ref, x_ref, y_ref, h_ref, e_ref, fp_ref, sp_ref, acc_ref)
    rho = rho_column(rho_ref, plan.paths, plan.stations)
    gains = solve(plan, acc_ref, anchor_ref[...], gain_ref[...], rho)
    gain_out[...] = gains
    total = residuals(plan, gains, msg_ref, ohp_ref, ohq_ref, x_out, y_out, h_out, e_out,
                      jp_ref, jq_ref)
    sum_ref[...] = jnp.broadcast_to(total, sum_ref.shape)


def last_kernel(rho_ref, gain_ref, anchor_ref, energy_ref, ohp_ref, ohq_ref,
                x_ref, y_ref, h_ref, e_ref,
                gain_out, fp_ref, sp_ref, acc_ref, *, plan, count):
    noise = noise_of(energy_ref[...], count)
    normal_sums(plan, noise, ohp_ref, ohq_ref, x_ref, y_ref, h_ref, e_ref, fp_ref, sp_ref, acc_ref)
    rho = rho_column(rho_ref, plan.paths, plan.stations)
    gain_out[...] = solve(plan, acc_ref, anchor_ref[...], gain_ref[...], rho)


def body(vis, model, pointing, pairs, gains, poly, dual, rhos, *, chans, blocks):
    paths, stations = gains.shape[2], gains.shape[3]
    sources, width = model.shape[2], model.shape[3]
    rows = COMPS * paths
    total_base = blocks * width
    total_ch = vis.shape[0] * chans
    plan = Plan(paths, stations, blocks, width)
    count = float(total_ch * total_base)
    own = plan.own
    block_start = lax.axis_index("stn") * own
    basis = basis_table(total_ch)
    mine = lax.dynamic_slice_in_dim(basis, lax.axis_index("chan"), 1, 0)[0]

    msg_rows = rows + COMPS + 8
    msg = pl.pallas_call(
        partial(combine_kernel, paths=paths, comps=sources),
        out_shape=jax.ShapeDtypeStruct((msg_rows, width), f32),
        in_specs=[SM, VM, VM, VM],
        out_specs=VM,
        compiler_params=params(),
        name="combine",
    )(pointing[:, 0], model.reshape(COMPS * sources, width), vis[0], pairs)

    own_at = lax.axis_index("stn")
    whole = jnp.zeros((msg_rows, total_base), f32)
    whole = lax.dynamic_update_slice(whole, msg, (0, own_at * width))
    for d in range(1, blocks):
        got = lax.ppermute(msg, "stn", [(i, (i + d) % blocks) for i in range(blocks)])
        whole = lax.dynamic_update_slice(whole, got, (0, (own_at - d) % blocks * width))

    def shape(*dims, dtype=f32):
        return jax.ShapeDtypeStruct(dims, dtype)

    state = [shape(rows, total_base)] * 3 + [shape(8, total_base), shape(8, LANES)]
    gather_scratch = [pltpu.VMEM((rows, width), f32)] * 2
    sum_scratch = [pltpu.VMEM((24 * paths, width), bf16)] * 2 + [pltpu.VMEM((12 * paths, stations), f32)]

    gain_now = gains.reshape(rows, stations)
    dual_now = dual.reshape(rows, stations)
    ohp, ohq, x, y, h, e, energy = pl.pallas_call(
        partial(first_kernel, plan=plan),
        out_shape=[shape(plan.window, total_base, dtype=bf16), shape(stations, total_base, dtype=bf16)] + state,
        in_specs=[VM, VM],
        out_specs=[VM] * 7,
        scratch_shapes=gather_scratch,
        compiler_params=params(40 << 20),
        name="first",
    )(gain_now, whole)

    def exchange(array):
        return lax.all_to_all(jnp.broadcast_to(array[None], (chans,) + array.shape), "chan", 0, 0)

    poly_now = poly.reshape(TERMS, rows, stations)
    consensus = sum(mine[t] * poly_now[t] for t in range(TERMS))
    anchor = consensus - dual_now
    steps = STEPS * INNER
    for n in range(steps):
        got = exchange(energy).reshape(chans * 8, LANES)[::8]
        if n < steps - 1:
            gain_now, x, y, h, e, energy = pl.pallas_call(
                partial(middle_kernel, plan=plan, count=count),
                out_shape=[shape(rows, stations)] + state,
                in_specs=[SM] + [VM] * 10,
                out_specs=[VM] * 6,
                scratch_shapes=gather_scratch + sum_scratch,
                compiler_params=params(40 << 20),
                name="middle",
            )(rhos, gain_now, anchor, got, whole, ohp, ohq, x, y, h, e)
        else:
            gain_now = pl.pallas_call(
                partial(last_kernel, plan=plan, count=count),
                out_shape=shape(rows, stations),
                in_specs=[SM] + [VM] * 9,
                out_specs=VM,
                scratch_shapes=sum_scratch,
                compiler_params=params(40 << 20),
                name="last",
            )(rhos, gain_now, anchor, got, ohp, ohq, x, y, h, e)
        if n % INNER == INNER - 1:
            tilted = gain_now + dual_now
            if n == steps - 1:
                tilted = lax.dynamic_slice(tilted, (0, block_start), (rows, own))
                gain_own = lax.dynamic_slice(gain_now, (0, block_start), (rows, own))
            all_ch = exchange(tilted)
            fit = [
                sum(basis[f, t] * all_ch[f] for f in range(total_ch)) / total_ch
                for t in range(TERMS)
            ]
            consensus = sum(mine[t] * fit[t] for t in range(TERMS))
            dual_now = tilted - consensus
            anchor = consensus - dual_now
    out = (1, COMPS, paths, own)
    return (
        gain_own.reshape(out),
        dual_now.reshape(out),
        jnp.stack(fit, axis=0).reshape((TERMS,) + out[1:]),
    )


def solution(mesh):
    placed = (
        P("chan", None, "stn"),
        P("chan", None, None, "stn"),
        P(),
        P(None, "stn"),
        P("chan", None, None, None),
        P(),
        P("chan", None, None, None),
        P(),
    )
    return jax.shard_map(
        partial(body, chans=mesh.shape["chan"], blocks=mesh.shape["stn"]),
        mesh=mesh,
        in_specs=placed,
        out_specs=(
            P("chan", None, None, "stn"),
            P("chan", None, None, "stn"),
            P(None, None, None, "stn"),
        ),
        check_vma=False,
    )
```

```python
from functools import partial

import jax
import jax.numpy as jnp
import numpy as np
from jax import lax
from jax.experimental import pallas as pl
from jax.experimental.pallas import tpu as pltpu
from jax.sharding import PartitionSpec as P

TERMS = 3
STEPS = 2
INNER = 2
COMPS = 8
LANES = 128

student_nu = 2.0
squared_tolerance = 1e-06
f32 = jnp.float32
bf16 = jnp.bfloat16


def cmul(a, b):
    return (a[0] * b[0] - a[1] * b[1], a[0] * b[1] + a[1] * b[0])


def cadd(a, b):
    return (a[0] + b[0], a[1] + b[1])


def conj(a):
    return (a[0], -a[1])


def mmul(a, b):
    return [
        cadd(cmul(a[0], b[0]), cmul(a[1], b[2])),
        cadd(cmul(a[0], b[1]), cmul(a[1], b[3])),
        cadd(cmul(a[2], b[0]), cmul(a[3], b[2])),
        cadd(cmul(a[2], b[1]), cmul(a[3], b[3])),
    ]


def adj(m):
    return [conj(m[0]), conj(m[2]), conj(m[1]), conj(m[3])]


def flat(m):
    return [m[i][0] for i in range(4)] + [m[i][1] for i in range(4)]


def square(a):
    return a[0] * a[0] + a[1] * a[1]


def gram(m):
    cross = cadd(cmul(m[0], conj(m[2])), cmul(m[1], conj(m[3])))
    return [
        square(m[0]) + square(m[1]),
        square(m[2]) + square(m[3]),
        cross[0],
        cross[1],
    ]


def basis_table(channel_count):
    frequency = (2.0 * np.arange(channel_count) + 1.0) / channel_count - 1.0
    columns = []
    for degree in range(TERMS):
        column = frequency**degree
        for earlier in columns:
            column = column - np.sum(earlier * column) / channel_count * earlier
        columns.append(column / np.sqrt(np.sum(column * column) / channel_count))
    return np.stack(columns, axis=1).astype(np.float32)


def split(x):
    hi = x.astype(bf16)
    lo = (x - hi.astype(f32)).astype(bf16)
    return hi, lo


def load(ref, paths, lanes):
    rows = [ref[c * paths : (c + 1) * paths, lanes] for c in range(COMPS)]
    return [(rows[i], rows[4 + i]) for i in range(4)]


class Plan:
    def __init__(self, paths, stations, blocks, chans, width):
        self.paths, self.stations = paths, stations
        self.blocks, self.width, self.chans = blocks, width, chans
        self.rows = COMPS * paths
        self.own = stations // blocks
        self.window = min(stations, max(self.own, LANES))
        self.centre = max(blocks // 2 - 1, 0)
        self.order = [i for i in range(blocks) if i != self.centre]

    def mirror(self, i):
        return self.blocks - 1 - i

    def inward(self):
        low, high = self.centre, self.mirror(self.centre)
        if low == high:
            return []
        return [[(i, low), (self.mirror(i), high)] for i in self.order]

    def outward(self):
        low, high = self.centre, self.mirror(self.centre)
        return [[(low, low - i), (high, high + i)] for i in range(1, self.centre + 1)]

    def slots(self):
        low = [[z] + self.order for z in range((self.blocks + 1) // 2)]
        high = [[z] + [self.mirror(i) for i in self.order] for z in range((self.blocks + 1) // 2, self.blocks)]
        return np.asarray(low + high, np.int32)


def radices(count):
    out = []
    while count > 1:
        step = 2 if not out and (count.bit_length() - 1) % 2 else 4
        out.append(step)
        count //= step
    return out


def partners(count, distance):
    return [(i, i ^ distance) for i in range(count)]


def chan_sum(x, count):
    span = 1
    for radix in radices(count):
        got = [lax.ppermute(x, "chan", partners(count, d * span)) for d in range(1, radix)]
        for y in got:
            x = x + y
        span *= radix
    return x


def chan_gather(x, count):
    x = x[None]
    span = 1
    for radix in radices(count):
        got = [lax.ppermute(x, "chan", partners(count, d * span)) for d in range(1, radix)]
        x = jnp.concatenate([x] + got, axis=0)
        span *= radix
    return x


def combine_kernel(point_ref, model_hbm, vis_hbm, pair_hbm, out_ref, model_ref, vis_ref, pair_ref,
                   sems, *, paths, comps):
    copies = [
        pltpu.make_async_copy(model_hbm, model_ref, sems.at[0]),
        pltpu.make_async_copy(vis_hbm, vis_ref, sems.at[1]),
        pltpu.make_async_copy(pair_hbm, pair_ref, sems.at[2]),
    ]
    for copy in copies:
        copy.start()
    for copy in copies:
        copy.wait()
    width = out_ref.shape[1]
    which = lax.broadcasted_iota(jnp.int32, (paths, width), 0)
    for c in range(COMPS):
        total = jnp.zeros((paths, width), f32)
        for s in range(comps):
            row = model_ref[c * comps + s : c * comps + s + 1, :]
            total = total + jnp.where(which == point_ref[s], row, 0.0)
        out_ref[c * paths : (c + 1) * paths, :] = total
    base = COMPS * paths
    out_ref[base : base + COMPS, :] = vis_ref[...]
    out_ref[base + COMPS : base + COMPS + 2, :] = pair_ref[...].astype(f32)
    out_ref[base + COMPS + 2 :, :] = jnp.zeros((6, width), f32)


def window_of(plan, starts_ref, slot):
    return pl.ds(pl.multiple_of(starts_ref[slot], LANES if plan.window % LANES == 0 else plan.window), plan.window)


def make_onehots(plan, starts_ref, msg_refs, ohp_ref, ohq_ref):
    width, base = plan.width, plan.rows + COMPS
    for i, msg_ref in enumerate(msg_refs):
        lanes = slice(i * width, (i + 1) * width)
        first = msg_ref[base : base + 1, :].astype(jnp.int32) - starts_ref[i]
        second = msg_ref[base + 1 : base + 2, :].astype(jnp.int32)
        pos = lax.broadcasted_iota(jnp.int32, (plan.window, width), 0)
        ohp_ref[:, lanes] = jnp.where(pos == first, 1.0, 0.0).astype(bf16)
        pos = lax.broadcasted_iota(jnp.int32, (plan.stations, width), 0)
        ohq_ref[:, lanes] = jnp.where(pos == second, 1.0, 0.0).astype(bf16)


def residuals(plan, starts_ref, gains, msg_refs, ohp_ref, ohq_ref, keep, both_ref, jp_ref, jq_ref):
    paths, rows, width = plan.paths, plan.rows, plan.width
    hi, lo = split(gains)
    both_ref[0:rows, :] = hi
    both_ref[rows : 2 * rows, :] = lo
    total = jnp.zeros((1, LANES), f32)
    for i, msg_ref in enumerate(msg_refs):
        block = slice(i * width, (i + 1) * width)
        got = jnp.dot(both_ref[...], ohq_ref[:, block], preferred_element_type=f32)
        jq_ref[...] = got[:rows] + got[rows:]
        near = both_ref[:, window_of(plan, starts_ref, i)]
        got = jnp.dot(near, ohp_ref[:, block], preferred_element_type=f32)
        jp_ref[...] = got[:rows] + got[rows:]

        def piece(t, carry):
            here = pl.ds(pl.multiple_of(t * LANES, LANES), LANES)
            there = pl.ds(pl.multiple_of(i * width + t * LANES, LANES), LANES)
            coherent = load(msg_ref, paths, here)
            y = mmul(coherent, adj(load(jq_ref, paths, here)))
            first = load(jp_ref, paths, here)
            g = flat(mmul(first, y))
            energy = jnp.zeros((1, LANES), f32)
            for c in range(COMPS):
                r = msg_ref[rows + c : rows + c + 1, here] - jnp.sum(g[c], axis=0, keepdims=True)
                energy = energy + r * r
                if keep is not None:
                    keep[0][c * paths : (c + 1) * paths, there] = r + g[c]
            if keep is not None:
                for c, v in enumerate(flat(y)):
                    keep[1][c * paths : (c + 1) * paths, there] = v
                for c, v in enumerate(flat(mmul(first, coherent))):
                    keep[2][c * paths : (c + 1) * paths, there] = v
                keep[3][0:1, there] = energy
            return carry + energy

        total = lax.fori_loop(0, width // LANES, piece, total)
    return total


def normal_sums(plan, starts_ref, noise, ohp_ref, ohq_ref, keep, fp_ref, sp_ref, acc_ref):
    paths, width = plan.paths, plan.width
    half = 12 * paths
    contract = (((1,), (1,)), ((), ()))
    x_ref, y_ref, h_ref, e_ref = keep
    for i in range(plan.blocks):
        block = slice(i * width, (i + 1) * width)

        def piece(t, carry):
            here = pl.ds(pl.multiple_of(t * LANES, LANES), LANES)
            there = pl.ds(pl.multiple_of(i * width + t * LANES, LANES), LANES)
            weight = (student_nu + 2.0) / (student_nu + e_ref[0:1, there] / noise)
            weight = jnp.broadcast_to(weight, (paths, LANES))
            x = [(a * weight, b * weight) for a, b in load(x_ref, paths, there)]
            y = load(y_ref, paths, there)
            parts = [v * weight for v in gram(y)] + flat(mmul(x, adj(y)))
            hi, lo = split(jnp.concatenate(parts, axis=0))
            fp_ref[0:half, here] = hi
            fp_ref[half : 2 * half, here] = lo
            h = load(h_ref, paths, there)
            parts = [v * weight for v in gram(adj(h))] + flat(mmul(adj(x), h))
            hi, lo = split(jnp.concatenate(parts, axis=0))
            sp_ref[0:half, here] = hi
            sp_ref[half : 2 * half, here] = lo
            return carry

        lax.fori_loop(0, width // LANES, piece, 0)
        got = lax.dot_general(sp_ref[...], ohq_ref[:, block], contract, preferred_element_type=f32)
        got = got[:half] + got[half:]
        if i == 0:
            acc_ref[...] = got
        else:
            acc_ref[...] += got
        got = lax.dot_general(fp_ref[...], ohp_ref[:, block], contract, preferred_element_type=f32)
        acc_ref[:, window_of(plan, starts_ref, i)] += got[:half] + got[half:]


def solve(plan, acc_ref, anchor, gains, rho_ref):
    paths = plan.paths
    which = lax.broadcasted_iota(jnp.int32, (paths, plan.stations), 0)
    rho = jnp.zeros((paths, plan.stations), f32)
    for k in range(paths):
        rho = jnp.where(which == k, rho_ref[k], rho)
    part = [acc_ref[c * paths : (c + 1) * paths, :] for c in range(12)]
    a, d = part[0] + rho, part[1] + rho
    inv = 1.0 / (a * d - part[2] * part[2] - part[3] * part[3])
    a, d, c0, c1 = a * inv, d * inv, part[2] * inv, part[3] * inv
    rhs = [part[4 + c] + rho * anchor[c * paths : (c + 1) * paths] for c in range(COMPS)]
    out = [None] * COMPS
    for row in (0, 2):
        u = (rhs[row], rhs[4 + row])
        v = (rhs[row + 1], rhs[5 + row])
        left = cmul(v, (c0, -c1))
        right = cmul(u, (c0, c1))
        out[row], out[4 + row] = u[0] * d - left[0], u[1] * d - left[1]
        out[row + 1], out[5 + row] = v[0] * a - right[0], v[1] * a - right[1]
    return 0.5 * (gains + jnp.concatenate(out, axis=0))


def noise_of(energy, count):
    per_lane = jnp.sum(energy, axis=0, keepdims=True)
    return jnp.sum(per_lane, axis=1, keepdims=True) / count + squared_tolerance


def fit_of(plan, basis_ref, index, fields):
    return [
        sum(basis_ref[lax.bitwise_xor(index, d), t] * field for d, field in enumerate(fields))
        / plan.chans
        for t in range(TERMS)
    ]


def consensus_of(basis_ref, index, fit):
    return sum(basis_ref[index, t] * fit[t] for t in range(TERMS))


def local_kernel(starts_ref, gain_ref, msg_ref, sum_ref, ohp_ref, ohq_ref, both_ref, jp_ref, jq_ref, *, plan):
    make_onehots(plan, starts_ref, [msg_ref], ohp_ref, ohq_ref)
    total = residuals(plan, starts_ref, gain_ref[...], [msg_ref], ohp_ref, ohq_ref, None,
                      both_ref, jp_ref, jq_ref)
    put_sum(sum_ref, total)


def put_sum(sum_ref, total):
    sum_ref[...] = jnp.zeros(sum_ref.shape, f32)
    sum_ref[0:1, :] = total


def first_kernel(rho_ref, starts_ref, basis_ref, index_ref, gain_ref, poly_ref, dual_ref, energy_ref,
                 *refs, plan, count):
    msg_refs, refs = refs[: plan.blocks], refs[plan.blocks :]
    ohp_ref, ohq_ref, gain_out, *refs = refs
    keep, (sum_ref, both_ref, jp_ref, jq_ref, fp_ref, sp_ref, acc_ref) = refs[:4], refs[4:]
    make_onehots(plan, starts_ref, msg_refs, ohp_ref, ohq_ref)
    gather = (msg_refs, ohp_ref, ohq_ref, keep, both_ref, jp_ref, jq_ref)
    residuals(plan, starts_ref, gain_ref[...], *gather)
    noise = noise_of(energy_ref[...], count)
    normal_sums(plan, starts_ref, noise, ohp_ref, ohq_ref, keep, fp_ref, sp_ref, acc_ref)
    anchor = consensus_of(basis_ref, index_ref[0], [poly_ref[t] for t in range(TERMS)]) - dual_ref[...]
    gains = solve(plan, acc_ref, anchor, gain_ref[...], rho_ref)
    gain_out[...] = gains
    put_sum(sum_ref, residuals(plan, starts_ref, gains, *gather))


def turn_kernel(rho_ref, starts_ref, basis_ref, index_ref, gain_ref, poly_ref, dual_ref, energy_ref,
                ohp_ref, ohq_ref, *refs, plan, count):
    keep, (gain_out, tilt_out, fp_ref, sp_ref, acc_ref) = refs[:4], refs[4:]
    noise = noise_of(energy_ref[...], count)
    normal_sums(plan, starts_ref, noise, ohp_ref, ohq_ref, keep, fp_ref, sp_ref, acc_ref)
    anchor = consensus_of(basis_ref, index_ref[0], [poly_ref[t] for t in range(TERMS)]) - dual_ref[...]
    gains = solve(plan, acc_ref, anchor, gain_ref[...], rho_ref)
    gain_out[...] = gains
    tilt_out[...] = gains + dual_ref[...]


def residual_kernel(starts_ref, gain_ref, ohp_ref, ohq_ref, *refs, plan):
    msg_refs, refs = refs[: plan.blocks], refs[plan.blocks :]
    keep, (sum_ref, both_ref, jp_ref, jq_ref) = refs[:4], refs[4:]
    put_sum(sum_ref, residuals(plan, starts_ref, gain_ref[...], msg_refs, ohp_ref, ohq_ref, keep,
                               both_ref, jp_ref, jq_ref))


def normal_kernel(starts_ref, energy_ref, ohp_ref, ohq_ref, *refs, plan, count):
    keep, (acc_ref, fp_ref, sp_ref) = refs[:4], refs[4:]
    noise = noise_of(energy_ref[...], count)
    normal_sums(plan, starts_ref, noise, ohp_ref, ohq_ref, keep, fp_ref, sp_ref, acc_ref)


def resume_kernel(rho_ref, starts_ref, basis_ref, index_ref, gain_ref, field_ref, acc_ref, ohp_ref, ohq_ref,
                  *refs, plan):
    msg_refs, refs = refs[: plan.blocks], refs[plan.blocks :]
    gain_out, dual_out, *refs = refs
    keep, (sum_ref, both_ref, jp_ref, jq_ref) = refs[:4], refs[4:]
    fit = fit_of(plan, basis_ref, index_ref[0], [field_ref[d] for d in range(plan.chans)])
    consensus = consensus_of(basis_ref, index_ref[0], fit)
    dual = field_ref[0] - consensus
    dual_out[...] = dual
    gains = solve(plan, acc_ref, consensus - dual, gain_ref[...], rho_ref)
    gain_out[...] = gains
    put_sum(sum_ref, residuals(plan, starts_ref, gains, msg_refs, ohp_ref, ohq_ref, keep,
                               both_ref, jp_ref, jq_ref))


def last_kernel(rho_ref, starts_ref, basis_ref, index_ref, gain_ref, field_ref, dual_ref, energy_ref,
                ohp_ref, ohq_ref, *refs, plan, count):
    keep, refs = refs[:4], refs[4:]
    outs, (fp_ref, sp_ref, acc_ref) = refs[:-3], refs[-3:]
    noise = noise_of(energy_ref[...], count)
    normal_sums(plan, starts_ref, noise, ohp_ref, ohq_ref, keep, fp_ref, sp_ref, acc_ref)
    fit = fit_of(plan, basis_ref, index_ref[0], [field_ref[d] for d in range(plan.chans)])
    consensus = consensus_of(basis_ref, index_ref[0], fit)
    gains = solve(plan, acc_ref, consensus - dual_ref[...], gain_ref[...], rho_ref)
    tilted = gains + dual_ref[...]
    rows, own = plan.rows, plan.own
    for n, out_ref in enumerate(outs):
        block = index_ref[1] + n * index_ref[2]
        for b in range(plan.blocks):

            @pl.when(block == b)
            def _():
                out_ref[0:rows, :] = gains[:, b * own : (b + 1) * own]
                out_ref[rows : 2 * rows, :] = tilted[:, b * own : (b + 1) * own]


def final_kernel(basis_ref, index_ref, field_ref, fit_out, dual_out, *, plan):
    fit = fit_of(plan, basis_ref, index_ref[0], [field_ref[d] for d in range(plan.chans)])
    for t in range(TERMS):
        fit_out[t] = fit[t]
    dual_out[...] = field_ref[0] - consensus_of(basis_ref, index_ref[0], fit)


VM = pl.BlockSpec(memory_space=pltpu.VMEM)
SM = pl.BlockSpec(memory_space=pltpu.SMEM)
ANY = pl.BlockSpec(memory_space=pl.ANY)


def shape(*dims, dtype=f32):
    return jax.ShapeDtypeStruct(dims, dtype)


def call(kernel, name, smem, arrays, outs, scratch, flops, limit=8 << 20, any_space=False):
    return pl.pallas_call(
        kernel,
        out_shape=outs,
        in_specs=[SM] * len(smem) + [ANY if any_space else VM] * len(arrays),
        out_specs=jax.tree.map(lambda _: VM, outs),
        scratch_shapes=scratch,
        compiler_params=pltpu.CompilerParams(vmem_limit_bytes=limit),
        cost_estimate=pl.CostEstimate(flops=flops, bytes_accessed=1 << 20, transcendentals=0),
        name=name,
    )(*smem, *arrays)


def body(vis, model, pointing, pairs, gains, poly, dual, rhos, *, chans, blocks):
    paths, stations = gains.shape[2], gains.shape[3]
    sources, width = model.shape[2], model.shape[3]
    plan = Plan(paths, stations, blocks, chans, width)
    rows, own = plan.rows, plan.own
    total_base = blocks * width
    count = float(chans * total_base)
    me, z = lax.axis_index("chan"), lax.axis_index("stn")
    basis = jnp.asarray(basis_table(chans))
    slots = jnp.asarray(plan.slots())[z]
    starts = slots * own // plan.window * plan.window
    outward = jnp.where(z <= plan.centre, -1, 1)
    index = jnp.stack([me, z, outward]).astype(jnp.int32)
    tables = (rhos, starts, basis, index)

    msg_rows = rows + COMPS + 8
    msg = call(
        partial(combine_kernel, paths=paths, comps=sources), "combine",
        (pointing[:, 0],), (model.reshape(COMPS * sources, width), vis[0], pairs),
        shape(msg_rows, width),
        [pltpu.VMEM((COMPS * sources, width), f32), pltpu.VMEM((COMPS, width), f32),
         pltpu.VMEM((2, width), jnp.int32), pltpu.SemaphoreType.DMA((3,))],
        1 << 24, any_space=True,
    )
    msgs = [msg] + [lax.ppermute(msg, "stn", pairs_of) for pairs_of in plan.inward()]

    tile = shape(8, LANES)
    keep = [shape(rows, total_base)] * 3 + [shape(8, total_base)]
    gather_scratch = [pltpu.VMEM((2 * rows, stations), bf16)] + [pltpu.VMEM((rows, width), f32)] * 2
    parts_scratch = [pltpu.VMEM((24 * paths, width), bf16)] * 2
    acc_scratch = [pltpu.VMEM((12 * paths, stations), f32)]
    acc_shape = shape(12 * paths, stations)
    field = shape(rows, stations)
    work = 1 << 31

    gain = gains.reshape(rows, stations)
    dual = dual.reshape(rows, stations)
    poly = poly.reshape(TERMS, rows, stations)
    energy = call(
        partial(local_kernel, plan=plan), "local", (starts,), (gain, msg), tile,
        [pltpu.VMEM((plan.window, width), bf16), pltpu.VMEM((stations, width), bf16)] + gather_scratch,
        work // 8,
    )
    energy = chan_sum(energy, chans)
    energy = jnp.concatenate(
        [energy] + [lax.ppermute(energy, "stn", pairs_of) for pairs_of in plan.inward()], axis=0
    )
    ohp, ohq, gain, *state, energy = call(
        partial(first_kernel, plan=plan, count=count), "first", tables,
        (gain, poly, dual, energy, *msgs),
        [shape(plan.window, total_base, dtype=bf16), shape(stations, total_base, dtype=bf16), field]
        + keep + [tile],
        gather_scratch + parts_scratch + acc_scratch, 3 * work,
    )
    gain, tilted = call(
        partial(turn_kernel, plan=plan, count=count), "turn", tables,
        (gain, poly, dual, chan_sum(energy, chans), ohp, ohq, *state),
        [field, field], parts_scratch + acc_scratch, work,
    )
    *state, energy = call(
        partial(residual_kernel, plan=plan), "residual", (starts,), (gain, ohp, ohq, *msgs),
        keep + [tile], gather_scratch, work,
    )
    fields = chan_gather(tilted, chans)
    acc = call(
        partial(normal_kernel, plan=plan, count=count), "normal", (starts,),
        (chan_sum(energy, chans), ohp, ohq, *state), acc_shape, parts_scratch, work,
    )
    gain, dual, *state, energy = call(
        partial(resume_kernel, plan=plan), "resume", tables, (gain, fields, acc, ohp, ohq, *msgs),
        [field, field] + keep + [tile], gather_scratch, work,
    )
    pieces = call(
        partial(last_kernel, plan=plan, count=count), "last", tables,
        (gain, fields, dual, chan_sum(energy, chans), ohp, ohq, *state),
        [shape(2 * rows, own)] * (plan.centre + 1), parts_scratch + acc_scratch, work,
    )
    mine = pieces[0]
    for n, pairs_of in enumerate(plan.outward(), 1):
        got = lax.ppermute(pieces[n], "stn", pairs_of)
        away = jnp.where(z <= plan.centre, plan.centre - z, z - plan.mirror(plan.centre))
        mine = jnp.where(away == n, got, mine)
    gain, tilted = mine[:rows], mine[rows:]
    fit, dual = call(
        partial(final_kernel, plan=plan), "final", (basis, index), (chan_gather(tilted, chans),),
        [shape(TERMS, rows, own), shape(rows, own)], [], 1 << 24,
    )
    out = (1, COMPS, paths, own)
    return gain.reshape(out), dual.reshape(out), fit.reshape((TERMS,) + out[1:])


def solution(mesh):
    placed = (
        P("chan", None, "stn"),
        P("chan", None, None, "stn"),
        P(),
        P(None, "stn"),
        P("chan", None, None, None),
        P(),
        P("chan", None, None, None),
        P(),
    )
    return jax.shard_map(
        partial(body, chans=mesh.shape["chan"], blocks=mesh.shape["stn"]),
        mesh=mesh,
        in_specs=placed,
        out_specs=(
            P("chan", None, None, "stn"),
            P("chan", None, None, "stn"),
            P(None, None, None, "stn"),
        ),
        check_vma=False,
    )
```
